32 devices in a mesh: dp: 16 (over z, y, x), grp: 2 (over core).
Axes of the slice: x: 2, y: 2, z: 4, core: 2. Of those that a mesh axis runs over, the one named last changes fastest.
Arguments:
- embeds: bfloat16 [8192, 1024], P(('dp', 'grp')), may hold values from -7 to 7
- quality: float32 [8192], P(('dp', 'grp')), may hold values from 0.5 to 2
- domain_ids: int32 [8192], P(('dp', 'grp')), may hold values from 0 to 15, as said below
- domain_weight: float32 [16], replicated, may hold values from 0.5 to 2
- dest: int32 [8192], P(('dp', 'grp')), may hold values from 0 to 31, as said below
- counts: int32 [32], P(('dp', 'grp')), may hold values from 192 to 256, as said below
- winners: int32 [4], replicated, may hold values from 0 to 8191, as said below
Outputs:
- relaid: bfloat16 [16384, 1024], P(('dp', 'grp'))
- residual_gain: float32 [16384], P(('dp', 'grp'))
- chol_rows: float32 [4, 16384], P(None, ('dp', 'grp'))
The draws below stay inside these ranges and needn't reach their ends.
Inputs may be any that keep to these rules, and one draw needn't show every extreme that they name: Rows 0 to counts - 1 of a device are valid, and one device has 256 valid rows. `dest`: destination device over dp and grp (index over dp+grp); among the valid rows of one device at most 16 name any one destination, and on every device some destination is named by exactly 16 valid rows. `domain_ids`: non-decreasing within each device's rows; a device's rows carry one domain number or two consecutive ones. `winners`: distinct valid rows, on distinct devices.
All inputs are finite; a program needn't handle non-finite values.
Results may differ from the reference program's by a relative error of at most 0.0048.
The reference program's roundings to bfloat16 on the way (of `row_quality` and `bal_quality`) count: a program that leaves them out, or rounds other values in their place, can miss the bound.
Values may be sent and summed in bfloat16 or wider, within the bound.
A program may use at most 64 MiB of HBM per device.

```python
import math
import jax
import jax.numpy as jnp
from jax import lax

D = 1024
DOMAINS = 16
STEPS = 4
SLOTS = 256
SHARDS = 32
CAP = 16
ROWS_BAL = 512
TOTAL_IN = 8192
TOTAL_OUT = 16384
N_DP = 16
N_GRP = 2


def device_counts(key):
    inner_key = jax.random.fold_in(key, 11)
    key_first, key_second = jax.random.split(inner_key)
    base_counts = jax.random.randint(key_first, (SHARDS,), SLOTS // 4 * 3, SLOTS + 1)
    busiest = jax.random.randint(key_second, (), 0, SHARDS)
    device_index = jnp.arange(SHARDS)
    full_rows = (device_index == busiest) | (device_index == SHARDS - 1)
    return jnp.where(full_rows, SLOTS, base_counts).astype(jnp.int32)


def domain_layout(key):
    inner_key = jax.random.fold_in(key, 13)
    lower_domain = jnp.arange(SHARDS) * DOMAINS // SHARDS
    upper_domain = jnp.minimum(lower_domain + 1, DOMAINS - 1)
    split_row = jax.random.randint(inner_key, (SHARDS, 1), 0, SLOTS + 1)
    column_index = jnp.arange(SLOTS)[None, :]
    layout = jnp.where(column_index >= split_row, upper_domain[:, None], lower_domain[:, None])
    return layout.reshape(-1).astype(jnp.int32)


def draw_counts(key, part):
    return device_counts(key)


def draw_domain_ids(key, part):
    return domain_layout(key)


def draw_embeds(key, part):
    inner_key = jax.random.fold_in(key, 17)
    key_list = jax.random.split(inner_key, 3)
    shared = jnp.clip(jax.random.normal(key_list[0], (D,), jnp.float32), -4.0, 4.0)
    centres = jnp.clip(jax.random.normal(key_list[1], (DOMAINS, D), jnp.float32), -4.0, 4.0)
    noise = jnp.clip(jax.random.normal(key_list[2], (SHARDS * SLOTS, D), jnp.float32), -4.0, 4.0)
    domains = domain_layout(key)
    values = 0.5 * shared[None, :] + 0.7 * centres[domains] + 0.5 * noise
    return values.astype(jnp.bfloat16)


def draw_dest(key, part):
    inner_key = jax.random.fold_in(key, 19)
    key_list = jax.random.split(inner_key, SHARDS)

    def one_device(device_key):
        key_first, key_second, key_third = jax.random.split(device_key, 3)
        target = jax.random.randint(key_first, (), 0, SHARDS)
        labels = (jnp.arange(SHARDS * CAP) // CAP + target) % SHARDS
        shuffled = jax.random.permutation(key_second, labels[CAP:])
        row_labels = jnp.concatenate([labels[:CAP], shuffled])[:SLOTS]
        head_part = jax.random.permutation(key_third, row_labels[:SLOTS // 4])
        return jnp.concatenate([head_part, row_labels[SLOTS // 4:]])
    return jax.vmap(one_device)(key_list).reshape(-1).astype(jnp.int32)


def draw_winners(key, part):
    valid_counts = device_counts(key)
    inner_key = jax.random.fold_in(key, 23)
    key_first, key_second, key_third = jax.random.split(inner_key, 3)
    middle = 1 + jax.random.permutation(key_first, SHARDS - 2)[:STEPS - 2]
    owners = jnp.concatenate([jnp.array([0, SHARDS - 1], jnp.int32), middle.astype(jnp.int32)])
    random_rows = jax.random.randint(key_second, (STEPS,), 0, valid_counts[owners])
    position = jnp.arange(STEPS)
    picked_rows = jnp.where(position == 0, 0, jnp.where(position == 1, SLOTS - 1, random_rows))
    order = jax.random.permutation(key_third, STEPS)
    return (owners * SLOTS + picked_rows)[order].astype(jnp.int32)


def shard_levels(own_key, extent, pieces, least, top_value):
    level = 1.0
    for axis_at, shards_of in pieces:
        draws = jax.random.uniform(jax.random.fold_in(jax.random.fold_in(own_key, 6), axis_at), (shards_of,), jnp.float32, least / len(pieces), top_value / len(pieces))
        level = level * jnp.repeat(jnp.exp(draws), extent[axis_at] // shards_of).reshape((-1,) + (1,) * (len(extent) - 1 - axis_at))
    return level


def setup_inputs(seed: int = 0) -> dict:
    arg_keys = jax.random.split(jax.random.key(seed), 8)
    embeds = draw_embeds(jax.random.fold_in(arg_keys[7], 71), 0)
    quality = jnp.clip(jnp.exp(math.log(2.0) - 1.3862944 * jax.random.uniform(arg_keys[1], (TOTAL_IN,), jnp.float32) ** shard_levels(arg_keys[1], (TOTAL_IN,), ((0, 32),), -0.2, 0.2)), 0.5, 2.0)
    domain_ids = draw_domain_ids(jax.random.fold_in(arg_keys[7], 71), 0)
    domain_weight = jnp.clip(jnp.exp(jax.random.uniform(arg_keys[3], (DOMAINS,), jnp.float32, math.log(0.5), math.log(2.0))), 0.5, 2.0)
    dest = draw_dest(jax.random.fold_in(arg_keys[7], 71), 0)
    counts = draw_counts(jax.random.fold_in(arg_keys[7], 71), 0)
    winners = draw_winners(jax.random.fold_in(arg_keys[7], 71), 0)
    return {"embeds": embeds, "quality": quality, "domain_ids": domain_ids, "domain_weight": domain_weight, "dest": dest, "counts": counts, "winners": winners}


RIDGE = 0.1

def reference(embeds, quality, domain_ids, domain_weight, dest, counts, winners):
    shards = N_DP * N_GRP
    row_quality = (quality * domain_weight[domain_ids]).astype(jnp.bfloat16)
    dest_grid = dest.reshape(shards, SLOTS)
    row_index = jnp.arange(SLOTS, dtype=jnp.int32)
    is_valid = row_index[None, :] < counts[:, None]
    targets = jnp.arange(shards, dtype=jnp.int32)

    def rank_rows(pair):
        dest_row, valid_row = pair
        dest_hot = ((dest_row[:, None] == targets[None, :]) & valid_row[:, None]).astype(jnp.int32)
        running = jnp.cumsum(dest_hot, axis=0) - dest_hot
        return lax.optimization_barrier(jnp.sum(running * dest_hot, axis=1)).astype(jnp.int32)
    dest_rank = lax.map(rank_rows, (dest_grid, is_valid))
    source_ids = jnp.arange(shards, dtype=jnp.int32)[:, None]
    bal_place = dest_grid * ROWS_BAL + source_ids * CAP + dest_rank
    bal_place = jnp.where(is_valid, bal_place, TOTAL_OUT).reshape(-1).astype(jnp.int32)
    relaid = jnp.zeros((TOTAL_OUT, D), jnp.bfloat16).at[bal_place].set(embeds, mode='drop')
    bal_quality = jnp.zeros((TOTAL_OUT,), jnp.bfloat16).at[bal_place].set(row_quality, mode='drop').astype(jnp.float32)
    win_rows = embeds[winners]
    win_place = bal_place[winners]
    blocks = relaid.reshape(shards, ROWS_BAL, D)

    def measure(block):
        row_norms = lax.optimization_barrier(jnp.sum(jnp.square(block.astype(jnp.float32)), axis=1))
        kernel_dots = lax.dot_general(win_rows, block, (((1,), (1,)), ((), ())), preferred_element_type=jnp.float32)
        return (row_norms, kernel_dots)
    row_norms, kernel_dots = lax.map(measure, blocks)
    row_norms = row_norms.reshape(-1)
    kernel_dots = jnp.transpose(kernel_dots, (1, 0, 2)).reshape(STEPS, TOTAL_OUT)
    residual_gain = jnp.where(bal_quality > 0, bal_quality * bal_quality * row_norms / D + RIDGE, 0.0)
    all_index = jnp.arange(TOTAL_OUT, dtype=jnp.int32)
    chol_rows = jnp.zeros((STEPS, TOTAL_OUT), jnp.float32)
    for turn_index in range(STEPS):
        target = win_place[turn_index]
        win_quality = bal_quality[target]
        ridge_hit = jnp.where(all_index == target, RIDGE, 0.0)
        column = bal_quality * win_quality * kernel_dots[turn_index] / D + ridge_hit
        win_chol = chol_rows[:, target]
        inner_sum = lax.optimization_barrier(jnp.sum(chol_rows * win_chol[:, None], axis=0))
        root_gain = jnp.sqrt(residual_gain[target])
        new_entry = (column - inner_sum) / root_gain
        chol_rows = chol_rows.at[turn_index].set(new_entry)
        residual_gain = residual_gain - new_entry * new_entry
    return (relaid, residual_gain, chol_rows)
```

```python
import functools
import jax
import jax.numpy as jnp
from jax import lax
from jax.experimental import pallas as pl
from jax.experimental.pallas import tpu as pltpu
from jax.sharding import PartitionSpec as P

RIDGE = 0.1
LANES = 128
MESH = pl.DeviceIdType.MESH


def flip(value, bits):
    out = 0
    weight = 1
    while weight <= bits:
        digit = (value // weight) % 2
        out = out + weight * ((1 - digit) if (bits // weight) % 2 else digit)
        weight *= 2
    return out + weight * (value // weight)


def kernel(
    sizes,
    embeds_hbm,
    quality_ref,
    domain_ref,
    dest_ref,
    weight_ref,
    counts_ref,
    winners_ref,
    relaid_hbm,
    gain_ref,
    chol_ref,
    embeds,
    send,
    recv,
    send_quality,
    recv_quality,
    send_winner,
    recv_winner,
    load_sem,
    send_sem,
    recv_sem,
    quality_sem,
    winner_sem,
    store_sem,
):
    pair_size, shards, slots, width, steps, domains = sizes
    per_pair = 2 * slots // shards
    balanced = shards * per_pair
    group = LANES // per_pair
    groups = shards // group
    me_dp = lax.axis_index("dp")
    me_grp = lax.axis_index("grp")
    me = me_dp * pair_size + me_grp
    my_group = me // group
    my_local = me % group

    load = pltpu.make_async_copy(embeds_hbm, embeds, load_sem)
    load.start()
    barrier = pltpu.get_barrier_semaphore()

    @pl.loop(1, shards)
    def _(k):
        peer = (me + k) % shards
        pl.semaphore_signal(
            barrier,
            inc=1,
            device_id=(peer // pair_size, peer % pair_size),
            device_id_type=MESH,
        )

    dest = dest_ref[...]
    row = lax.broadcasted_iota(jnp.int32, (1, slots), 1)
    valid = row < counts_ref[0]
    domain = domain_ref[...]
    weight = jnp.zeros((1, slots), jnp.float32)
    for d in range(domains):
        weight = jnp.where(domain == d, weight_ref[d], weight)
    quality = jnp.where(valid, quality_ref[...] * weight, 0.0)
    quality = quality.astype(jnp.bfloat16).astype(jnp.float32)
    target = lax.broadcasted_iota(jnp.int32, (shards, slots), 0)
    hot = (target == dest) & valid
    hot_wide = jnp.where(hot, 1.0, 0.0)
    before = jnp.where(
        lax.broadcasted_iota(jnp.int32, (slots, slots), 0)
        < lax.broadcasted_iota(jnp.int32, (slots, slots), 1),
        1.0,
        0.0,
    ).astype(jnp.bfloat16)
    earlier = jnp.dot(
        hot_wide.astype(jnp.bfloat16), before, preferred_element_type=jnp.float32
    )
    rank = jnp.sum(jnp.where(hot, earlier, 0.0), axis=0, keepdims=True)
    rank = rank.astype(jnp.int32)
    slot = jnp.where(valid, dest * per_pair + rank, -1)
    place = (dest * balanced + me * per_pair + rank).astype(jnp.float32)

    lane_rank = lax.broadcasted_iota(jnp.int32, (LANES, slots), 0)
    rank_hot = jnp.where(lane_rank == rank + my_local * per_pair, 1.0, 0.0)
    spread = lax.dot_general(
        jnp.where(hot, quality, 0.0).astype(jnp.bfloat16),
        rank_hot.astype(jnp.bfloat16),
        (((1,), (1,)), ((), ())),
        preferred_element_type=jnp.float32,
    )
    send_quality[...] = spread.reshape(shards, 1, LANES)

    chosen = row < 0
    lane = lax.broadcasted_iota(jnp.int32, (1, LANES), 1)
    meta = jnp.zeros((1, LANES), jnp.float32)
    for t in range(steps):
        local = winners_ref[t] - me * slots
        chosen_now = row == local
        chosen = chosen | chosen_now
        mine = jnp.where((local >= 0) & (local < slots), 1.0, 0.0)
        meta = jnp.where(lane == t, mine, meta)
    won_quality = jnp.sum(jnp.where(chosen, quality, 0.0), axis=1, keepdims=True)
    won_place = jnp.sum(jnp.where(chosen, place, 0.0), axis=1, keepdims=True)
    meta = jnp.where(lane == steps, won_quality, meta)
    meta = jnp.where(lane == steps + 1, won_place, meta)
    send_winner[:, width:] = meta
    load.wait()
    picked = jnp.dot(
        jnp.broadcast_to(jnp.where(chosen, 1.0, 0.0), (16, slots)).astype(jnp.bfloat16),
        embeds[...],
        preferred_element_type=jnp.float32,
    )
    send_winner[:, :width] = picked[0:1]

    slot_index = lax.broadcasted_iota(jnp.int32, (balanced, slots), 0)
    permute = jnp.where(slot_index == slot, 1.0, 0.0).astype(jnp.bfloat16)
    for c in range(0, width, 256):
        moved = jnp.dot(
            permute, embeds[:, c : c + 256], preferred_element_type=jnp.float32
        )
        send[:, :, c : c + 256] = moved.astype(jnp.bfloat16).reshape(shards, per_pair, 256)

    own_rows = pltpu.make_async_copy(send.at[me], recv.at[me], recv_sem.at[my_group])
    own_quality = pltpu.make_async_copy(
        send_quality.at[me], recv_quality.at[me], quality_sem.at[my_group]
    )
    own_winner = pltpu.make_async_copy(send_winner, recv_winner.at[me], winner_sem)

    pl.semaphore_wait(barrier, shards - 1)

    def peer_of(bits, k):
        peer = flip(my_group, bits) * group + (my_local + k) % group
        return peer, (peer // pair_size, peer % pair_size)

    def over_peers(fn):
        for bits in range(groups - 1, -1, -1):

            @pl.loop(0 if bits else 1, group)
            def _(k):
                fn(*peer_of(bits, k))

    def send_small(peer, device):
        pltpu.make_async_remote_copy(
            src_ref=send_winner,
            dst_ref=recv_winner.at[me],
            send_sem=send_sem.at[0],
            recv_sem=winner_sem,
            device_id=device,
            device_id_type=MESH,
        ).start()

    def send_rows(peer, device):
        pltpu.make_async_remote_copy(
            src_ref=send_quality.at[peer],
            dst_ref=recv_quality.at[me],
            send_sem=send_sem.at[1],
            recv_sem=quality_sem.at[my_group],
            device_id=device,
            device_id_type=MESH,
        ).start()
        pltpu.make_async_remote_copy(
            src_ref=send.at[peer],
            dst_ref=recv.at[me],
            send_sem=send_sem.at[2],
            recv_sem=recv_sem.at[my_group],
            device_id=device,
            device_id_type=MESH,
        ).start()

    over_peers(send_small)
    own_winner.start()
    over_peers(send_rows)
    own_rows.start()
    own_quality.start()

    pltpu.make_async_copy(recv_winner, recv_winner, winner_sem).wait()
    heard = recv_winner[...].reshape(shards, width + LANES)
    kept = []
    for t in range(steps):
        pick = heard[:, width + t : width + t + 1]
        kept.append(jnp.sum(heard * pick, axis=0, keepdims=True))
    step_row = lax.broadcasted_iota(jnp.int32, (16, width), 0)
    wins = jnp.zeros((16, width), jnp.float32)
    for t in range(steps):
        wins = jnp.where(step_row == t, kept[t][:, :width], wins)
    wins = wins.astype(jnp.bfloat16)
    gram = lax.dot_general(
        wins, wins, (((1,), (1,)), ((), ())), preferred_element_type=jnp.float32
    )
    win_quality = [kept[t][:, width + steps : width + steps + 1] for t in range(steps)]
    win_place = [kept[t][:, width + steps + 1 : width + steps + 2] for t in range(steps)]
    columns = []
    roots = []
    for t in range(steps):
        column = []
        for k in range(t):
            cross = win_quality[k] * win_quality[t] * gram[k : k + 1, t : t + 1] / width
            for e in range(k):
                cross = cross - columns[k][e] * column[e]
            column.append(cross / roots[k])
        left = win_quality[t] * win_quality[t] * gram[t : t + 1, t : t + 1] / width + RIDGE
        for k in range(t):
            left = left - column[k] * column[k]
        columns.append(column)
        roots.append(jnp.sqrt(left))

    for bits in range(groups):
        here = flip(my_group, bits)
        first = here * group
        blocks = recv.at[pl.ds(first, group)]
        scores = recv_quality.at[pl.ds(first, group)]
        pltpu.make_async_copy(blocks, blocks, recv_sem.at[here]).wait()
        pltpu.make_async_copy(scores, scores, quality_sem.at[here]).wait()
        pltpu.make_async_copy(
            blocks, relaid_hbm.at[pl.ds(first, group)], store_sem.at[bits]
        ).start()
        rows = blocks[...].reshape(LANES, width)
        bal_quality = jnp.sum(scores[...].reshape(group, LANES), axis=0, keepdims=True)
        dots = lax.dot_general(
            wins, rows, (((1,), (1,)), ((), ())), preferred_element_type=jnp.float32
        )
        total = jnp.zeros((LANES, LANES), jnp.float32)
        for c in range(0, width, LANES):
            part = rows[:, c : c + LANES].astype(jnp.float32)
            total = total + part * part
        norms = jnp.sum(total.T, axis=0, keepdims=True)
        gain = jnp.where(
            bal_quality > 0, bal_quality * bal_quality * norms / width + RIDGE, 0.0
        )
        at = (me * balanced + here * LANES + lane).astype(jnp.float32)
        span = pl.ds(pl.multiple_of(here * LANES, LANES), LANES)
        entries = []
        for t in range(steps):
            inner = jnp.zeros((1, LANES), jnp.float32)
            for k in range(t):
                inner = inner + entries[k] * columns[t][k]
            hit = jnp.where(at == win_place[t], RIDGE, 0.0)
            entry = (
                bal_quality * win_quality[t] * dots[t : t + 1] / width + hit - inner
            ) / roots[t]
            entries.append(entry)
            gain = gain - entry * entry
            chol_ref[t : t + 1, span] = entry
        gain_ref[:, span] = gain

    for bits in range(groups):
        blocks = recv.at[pl.ds(flip(my_group, bits) * group, group)]
        pltpu.make_async_copy(
            blocks, relaid_hbm.at[pl.ds(flip(my_group, bits) * group, group)], store_sem.at[bits]
        ).wait()
    others = recv_winner.at[pl.ds(0, shards - 1)]
    pltpu.make_async_copy(others, others, send_sem.at[0]).wait()
    others = send_quality.at[pl.ds(0, shards - 1)]
    pltpu.make_async_copy(others, others, send_sem.at[1]).wait()
    others = send.at[pl.ds(0, shards - 1)]
    pltpu.make_async_copy(others, others, send_sem.at[2]).wait()


def body(embeds, quality, domain_ids, domain_weight, dest, counts, winners):
    shards = lax.axis_size(("dp", "grp"))
    pair_size = lax.axis_size("grp")
    slots, width = embeds.shape
    steps = winners.shape[0]
    domains = domain_weight.shape[0]
    per_pair = 2 * slots // shards
    balanced = shards * per_pair
    groups = balanced // LANES
    vmem = pl.BlockSpec(memory_space=pltpu.VMEM)
    smem = pl.BlockSpec(memory_space=pltpu.SMEM)
    anywhere = pl.BlockSpec(memory_space=pl.ANY)
    dma = pltpu.SemaphoreType.DMA
    relaid, gain, chol = pl.pallas_call(
        functools.partial(kernel, (pair_size, shards, slots, width, steps, domains)),
        out_shape=(
            jax.ShapeDtypeStruct((shards, per_pair, width), jnp.bfloat16),
            jax.ShapeDtypeStruct((1, balanced), jnp.float32),
            jax.ShapeDtypeStruct((steps, balanced), jnp.float32),
        ),
        in_specs=[anywhere, vmem, vmem, vmem, smem, smem, smem],
        out_specs=(anywhere, vmem, vmem),
        scratch_shapes=[
            pltpu.VMEM((slots, width), jnp.bfloat16),
            pltpu.VMEM((shards, per_pair, width), jnp.bfloat16),
            pltpu.VMEM((shards, per_pair, width), jnp.bfloat16),
            pltpu.VMEM((shards, 1, LANES), jnp.float32),
            pltpu.VMEM((shards, 1, LANES), jnp.float32),
            pltpu.VMEM((1, width + LANES), jnp.float32),
            pltpu.VMEM((shards, 1, width + LANES), jnp.float32),
            dma,
            dma((3,)),
            dma((groups,)),
            dma((groups,)),
            dma,
            dma((groups,)),
        ],
        compiler_params=pltpu.CompilerParams(collective_id=0, has_side_effects=True),
        name="relay_select",
    )(
        embeds,
        quality.reshape(1, slots),
        domain_ids.reshape(1, slots),
        dest.reshape(1, slots),
        domain_weight,
        counts,
        winners,
    )
    return relaid.reshape(balanced, width), gain.reshape(balanced), chol


def solution(mesh):
    return jax.shard_map(
        body,
        mesh=mesh,
        in_specs=(
            P(("dp", "grp"), None),
            P(("dp", "grp")),
            P(("dp", "grp")),
            P(),
            P(("dp", "grp")),
            P(("dp", "grp")),
            P(),
        ),
        out_specs=(P(("dp", "grp"), None), P(("dp", "grp")), P(None, ("dp", "grp"))),
        check_vma=False,
    )
```

```python
import functools
import jax
import jax.numpy as jnp
from jax import lax
from jax.experimental import pallas as pl
from jax.experimental.pallas import tpu as pltpu
from jax.sharding import PartitionSpec as P

RIDGE = 0.1
LANES = 128
MESH = pl.DeviceIdType.MESH


def flip(value, bits):
    out = 0
    weight = 1
    while weight <= bits:
        digit = (value // weight) % 2
        out = out + weight * ((1 - digit) if (bits // weight) % 2 else digit)
        weight *= 2
    return out + weight * (value // weight)


def kernel(
    sizes,
    embeds_hbm,
    quality_ref,
    domain_ref,
    dest_ref,
    weight_ref,
    counts_ref,
    winners_ref,
    recv,
    result_ref,
    embeds,
    send,
    send_quality,
    recv_quality,
    send_winner,
    recv_winner,
    load_sem,
    send_sem,
    recv_sem,
    quality_sem,
    winner_sem,
    mate_sem,
):
    pair_size, shards, slots, width, steps, domains = sizes
    per_pair = 2 * slots // shards
    balanced = shards * per_pair
    spread_size = shards // pair_size
    group = LANES // per_pair
    groups = shards // group
    me_dp = lax.axis_index("dp")
    me_grp = lax.axis_index("grp")
    me = me_dp * pair_size + me_grp
    my_group = me // group
    my_local = me % group

    load = pltpu.make_async_copy(embeds_hbm, embeds, load_sem)
    load.start()
    barrier = pltpu.get_barrier_semaphore()

    @pl.loop(1, shards)
    def _(k):
        peer = (me + k) % shards
        pl.semaphore_signal(
            barrier,
            inc=1,
            device_id=(peer // pair_size, peer % pair_size),
            device_id_type=MESH,
        )

    dest = dest_ref[...]
    row = lax.broadcasted_iota(jnp.int32, (1, slots), 1)
    valid = row < counts_ref[0]
    domain = domain_ref[...]
    weight = jnp.zeros((1, slots), jnp.float32)
    for d in range(domains):
        weight = jnp.where(domain == d, weight_ref[d], weight)
    quality = jnp.where(valid, quality_ref[...] * weight, 0.0)
    quality = quality.astype(jnp.bfloat16).astype(jnp.float32)
    target = lax.broadcasted_iota(jnp.int32, (shards, slots), 0)
    hot = (target == dest) & valid
    hot_wide = jnp.where(hot, 1.0, 0.0)
    before = jnp.where(
        lax.broadcasted_iota(jnp.int32, (slots, slots), 0)
        < lax.broadcasted_iota(jnp.int32, (slots, slots), 1),
        1.0,
        0.0,
    ).astype(jnp.bfloat16)
    earlier = jnp.dot(
        hot_wide.astype(jnp.bfloat16), before, preferred_element_type=jnp.float32
    )
    rank = jnp.sum(jnp.where(hot, earlier, 0.0), axis=0, keepdims=True)
    rank = rank.astype(jnp.int32)
    slot = jnp.where(valid, dest * per_pair + rank, -1)
    place = (dest * balanced + me * per_pair + rank).astype(jnp.float32)

    lane_rank = lax.broadcasted_iota(jnp.int32, (LANES, slots), 0)
    rank_hot = jnp.where(lane_rank == rank + my_local * per_pair, 1.0, 0.0)
    spread = lax.dot_general(
        jnp.where(hot, quality, 0.0).astype(jnp.bfloat16),
        rank_hot.astype(jnp.bfloat16),
        (((1,), (1,)), ((), ())),
        preferred_element_type=jnp.float32,
    )

    chosen = row < 0
    lane = lax.broadcasted_iota(jnp.int32, (1, LANES), 1)
    lane_fact = (lane + (LANES - (my_local + 1) * per_pair)) % LANES
    meta = jnp.zeros((1, LANES), jnp.float32)
    for t in range(steps):
        local = winners_ref[t] - me * slots
        chosen_now = row == local
        chosen = chosen | chosen_now
        mine = jnp.where((local >= 0) & (local < slots), 1.0, 0.0)
        meta = jnp.where(lane_fact == t, mine, meta)
    won_quality = jnp.sum(jnp.where(chosen, quality, 0.0), axis=1, keepdims=True)
    won_place = jnp.sum(jnp.where(chosen, place, 0.0), axis=1, keepdims=True)
    meta = jnp.where(lane_fact == steps, won_quality, meta)
    meta = jnp.where(lane_fact == steps + 1, won_place, meta)
    send_quality[...] = (spread + meta).reshape(shards, 1, LANES)
    load.wait()
    picked = jnp.dot(
        jnp.broadcast_to(jnp.where(chosen, 1.0, 0.0), (16, slots)).astype(jnp.bfloat16),
        embeds[...],
        preferred_element_type=jnp.float32,
    )
    folds = width // LANES
    fold_row = lax.broadcasted_iota(jnp.int32, (folds, LANES), 0)
    folded = jnp.zeros((folds, LANES), jnp.float32)
    for f in range(folds):
        folded = jnp.where(
            fold_row == f, picked[0:1, f * LANES : (f + 1) * LANES], folded
        )
    send_winner[...] = folded.astype(jnp.bfloat16)

    slot_index = lax.broadcasted_iota(jnp.int32, (balanced, slots), 0)
    permute = jnp.where(slot_index == slot, 1.0, 0.0).astype(jnp.bfloat16)
    for c in range(0, width, 256):
        moved = jnp.dot(
            permute, embeds[:, c : c + 256], preferred_element_type=jnp.float32
        )
        send[:, :, c : c + 256] = moved.astype(jnp.bfloat16).reshape(shards, per_pair, 256)

    own_rows = pltpu.make_async_copy(send.at[me], recv.at[me], recv_sem.at[my_group])
    own_quality = pltpu.make_async_copy(
        send_quality.at[me], recv_quality.at[me], quality_sem.at[my_group]
    )
    own_winner = pltpu.make_async_copy(
        send_winner, recv_winner.at[me_grp, me_dp], winner_sem.at[0]
    )

    pl.semaphore_wait(barrier, shards - 1)

    @pl.loop(1, spread_size)
    def _(k):
        pltpu.make_async_remote_copy(
            src_ref=send_winner,
            dst_ref=recv_winner.at[me_grp, me_dp],
            send_sem=send_sem.at[0],
            recv_sem=winner_sem.at[0],
            device_id=((me_dp + k) % spread_size, me_grp),
            device_id_type=MESH,
        ).start()

    own_winner.start()

    def send_rows(bits, k):
        peer = flip(my_group, bits) * group + (my_local + k) % group
        device = (peer // pair_size, peer % pair_size)
        pltpu.make_async_remote_copy(
            src_ref=send_quality.at[peer],
            dst_ref=recv_quality.at[me],
            send_sem=send_sem.at[1],
            recv_sem=quality_sem.at[my_group],
            device_id=device,
            device_id_type=MESH,
        ).start()
        pltpu.make_async_remote_copy(
            src_ref=send.at[peer],
            dst_ref=recv.at[me],
            send_sem=send_sem.at[2],
            recv_sem=recv_sem.at[my_group],
            device_id=device,
            device_id_type=MESH,
        ).start()

    @pl.loop(0, group)
    def _(k):
        for bits in range(groups - 1, 0, -1):
            send_rows(bits, k)

        @pl.when(k > 0)
        def _():
            send_rows(0, k)

    own_rows.start()
    own_quality.start()

    mine = recv_winner.at[me_grp]
    pltpu.make_async_copy(mine, mine, winner_sem.at[0]).wait()
    relays = []
    for k in range(1, pair_size):
        relay = pltpu.make_async_remote_copy(
            src_ref=mine,
            dst_ref=mine,
            send_sem=mate_sem.at[0, k - 1],
            recv_sem=mate_sem.at[1, k - 1],
            device_id=(me_dp, (me_grp + k) % pair_size),
            device_id_type=MESH,
        )
        relay.start()
        relays.append(relay)
    for relay in relays:
        relay.wait()
    for g in range(groups):
        scores = recv_quality.at[pl.ds(g * group, group)]
        pltpu.make_async_copy(scores, scores, quality_sem.at[g]).wait()

    facts = recv_quality[...].reshape(shards, LANES)
    source = lax.broadcasted_iota(jnp.int32, (shards, LANES), 0)
    fact_lane = lax.broadcasted_iota(jnp.int32, (shards, LANES), 1)
    fact = (fact_lane + (LANES - (source % group + 1) * per_pair)) % LANES
    def fact_of(i):
        return jnp.sum(jnp.where(fact == i, facts, 0.0), axis=1, keepdims=True)

    owners = [fact_of(t) for t in range(steps)]
    source_quality = fact_of(steps)
    source_place = fact_of(steps + 1)
    win_quality = [jnp.sum(o * source_quality, axis=0, keepdims=True) for o in owners]
    win_place = [jnp.sum(o * source_place, axis=0, keepdims=True) for o in owners]
    owner_table = jnp.zeros((shards, LANES), jnp.float32)
    for t in range(steps):
        owner_table = jnp.where(fact_lane == t, owners[t], owner_table)
    line = lax.broadcasted_iota(jnp.int32, (shards, shards * folds), 1)
    order = line // folds
    line_source = (order % spread_size) * pair_size + order // spread_size
    line_hot = jnp.where(
        line_source == lax.broadcasted_iota(jnp.int32, line.shape, 0), 1.0, 0.0
    )
    spread_owner = jnp.dot(
        owner_table.T[:16].astype(jnp.bfloat16),
        line_hot.astype(jnp.bfloat16),
        preferred_element_type=jnp.float32,
    )
    lines = recv_winner[...].reshape(shards * folds, LANES)
    line_fold = lax.broadcasted_iota(jnp.int32, spread_owner.shape, 1) % folds
    wins = jnp.concatenate(
        [
            jnp.dot(
                jnp.where(line_fold == f, spread_owner, 0.0).astype(jnp.bfloat16),
                lines,
                preferred_element_type=jnp.float32,
            )
            for f in range(folds)
        ],
        axis=1,
    ).astype(jnp.bfloat16)
    gram = lax.dot_general(
        wins, wins, (((1,), (1,)), ((), ())), preferred_element_type=jnp.float32
    )
    columns = []
    roots = []
    for t in range(steps):
        column = []
        for k in range(t):
            cross = win_quality[k] * win_quality[t] * gram[k : k + 1, t : t + 1] / width
            for e in range(k):
                cross = cross - columns[k][e] * column[e]
            column.append(cross / roots[k])
        left = win_quality[t] * win_quality[t] * gram[t : t + 1, t : t + 1] / width + RIDGE
        for k in range(t):
            left = left - column[k] * column[k]
        columns.append(column)
        roots.append(jnp.sqrt(left))

    for bits in range(groups):
        here = flip(my_group, bits)
        first = here * group
        blocks = recv.at[pl.ds(first, group)]
        scores = recv_quality.at[pl.ds(first, group)]
        pltpu.make_async_copy(blocks, blocks, recv_sem.at[here]).wait()
        rows = blocks[...].reshape(LANES, width)
        own_lane = lax.broadcasted_iota(jnp.int32, (group, LANES), 1) // per_pair
        own_lane = own_lane == lax.broadcasted_iota(jnp.int32, (group, LANES), 0)
        bal_quality = jnp.sum(
            jnp.where(own_lane, scores[...].reshape(group, LANES), 0.0),
            axis=0,
            keepdims=True,
        )
        dots = lax.dot_general(
            wins, rows, (((1,), (1,)), ((), ())), preferred_element_type=jnp.float32
        )
        total = jnp.zeros((LANES, LANES), jnp.float32)
        for c in range(0, width, LANES):
            part = rows[:, c : c + LANES].astype(jnp.float32)
            total = total + part * part
        norms = jnp.sum(total.T, axis=0, keepdims=True)
        gain = jnp.where(
            bal_quality > 0, bal_quality * bal_quality * norms / width + RIDGE, 0.0
        )
        at = (me * balanced + here * LANES + lane).astype(jnp.float32)
        span = pl.ds(pl.multiple_of(here * LANES, LANES), LANES)
        entries = []
        for t in range(steps):
            inner = jnp.zeros((1, LANES), jnp.float32)
            for k in range(t):
                inner = inner + entries[k] * columns[t][k]
            hit = jnp.where(at == win_place[t], RIDGE, 0.0)
            entry = (
                bal_quality * win_quality[t] * dots[t : t + 1] / width + hit - inner
            ) / roots[t]
            entries.append(entry)
            gain = gain - entry * entry
            result_ref[t : t + 1, span] = entry
        result_ref[steps : steps + 1, span] = gain

    others = recv_winner.at[0, pl.ds(0, spread_size - 1)]
    pltpu.make_async_copy(others, others, send_sem.at[0]).wait()
    others = send_quality.at[pl.ds(0, shards - 1)]
    pltpu.make_async_copy(others, others, send_sem.at[1]).wait()
    others = send.at[pl.ds(0, shards - 1)]
    pltpu.make_async_copy(others, others, send_sem.at[2]).wait()


def write_kernel(steps, rows_ref, result_ref, relaid_hbm, gain_ref, chol_ref, sem):
    copy = pltpu.make_async_copy(rows_ref, relaid_hbm, sem)
    copy.start()
    gain_ref[...] = result_ref[steps : steps + 1]
    chol_ref[...] = result_ref[:steps]
    copy.wait()


def body(embeds, quality, domain_ids, domain_weight, dest, counts, winners):
    shards = lax.axis_size(("dp", "grp"))
    pair_size = lax.axis_size("grp")
    slots, width = embeds.shape
    steps = winners.shape[0]
    domains = domain_weight.shape[0]
    per_pair = 2 * slots // shards
    balanced = shards * per_pair
    groups = balanced // LANES
    vmem = pl.BlockSpec(memory_space=pltpu.VMEM)
    smem = pl.BlockSpec(memory_space=pltpu.SMEM)
    hbm = pl.BlockSpec(memory_space=pltpu.HBM)
    dma = pltpu.SemaphoreType.DMA
    folds = width // LANES
    rows, result = pl.pallas_call(
        functools.partial(kernel, (pair_size, shards, slots, width, steps, domains)),
        out_shape=(
            pltpu.VMEM((shards, per_pair, width), jnp.bfloat16),
            pltpu.VMEM((8, balanced), jnp.float32),
        ),
        in_specs=[hbm, vmem, vmem, vmem, smem, smem, smem],
        out_specs=(vmem, vmem),
        scratch_shapes=[
            pltpu.VMEM((slots, width), jnp.bfloat16),
            pltpu.VMEM((shards, per_pair, width), jnp.bfloat16),
            pltpu.VMEM((shards, 1, LANES), jnp.float32),
            pltpu.VMEM((shards, 1, LANES), jnp.float32),
            pltpu.VMEM((folds, LANES), jnp.bfloat16),
            pltpu.VMEM((pair_size, shards // pair_size, folds, LANES), jnp.bfloat16),
            dma,
            dma((3,)),
            dma((groups,)),
            dma((groups,)),
            dma((1,)),
            dma((2, pair_size - 1)),
        ],
        compiler_params=pltpu.CompilerParams(
            collective_id=0, has_side_effects=True, vmem_limit_bytes=24 * 1024 * 1024
        ),
        name="relay_select",
    )(
        embeds,
        quality.reshape(1, slots),
        domain_ids.reshape(1, slots),
        dest.reshape(1, slots),
        domain_weight,
        counts,
        winners,
    )
    relaid, gain, chol = pl.pallas_call(
        functools.partial(write_kernel, steps),
        out_shape=(
            jax.ShapeDtypeStruct((shards, per_pair, width), jnp.bfloat16),
            jax.ShapeDtypeStruct((1, balanced), jnp.float32),
            jax.ShapeDtypeStruct((steps, balanced), jnp.float32),
        ),
        in_specs=[vmem, vmem],
        out_specs=(hbm, vmem, vmem),
        scratch_shapes=[dma],
        compiler_params=pltpu.CompilerParams(vmem_limit_bytes=8 * 1024 * 1024),
        name="write_out",
    )(rows, result)
    return relaid.reshape(balanced, width), gain.reshape(balanced), chol


def solution(mesh):
    return jax.shard_map(
        body,
        mesh=mesh,
        in_specs=(
            P(("dp", "grp"), None),
            P(("dp", "grp")),
            P(("dp", "grp")),
            P(),
            P(("dp", "grp")),
            P(("dp", "grp")),
            P(),
        ),
        out_specs=(P(("dp", "grp"), None), P(("dp", "grp")), P(None, ("dp", "grp"))),
        check_vma=False,
    )
```

```python
import functools
import jax
import jax.numpy as jnp
from jax import lax
from jax.experimental import pallas as pl
from jax.experimental.pallas import tpu as pltpu
from jax.sharding import PartitionSpec as P

RIDGE = 0.1
VMEM_BYTES = 67043328
LANES = 128
MESH = pl.DeviceIdType.MESH


def flip(value, bits):
    out = 0
    weight = 1
    while weight <= bits:
        digit = (value // weight) % 2
        out = out + weight * ((1 - digit) if (bits // weight) % 2 else digit)
        weight *= 2
    return out + weight * (value // weight)


def kernel(
    sizes,
    embeds_hbm,
    quality_hbm,
    domain_hbm,
    dest_hbm,
    weight_hbm,
    counts_hbm,
    winners_hbm,
    recv,
    gain_ref,
    chol_ref,
    embeds,
    quality_ref,
    domain_ref,
    dest_ref,
    weight_ref,
    counts_ref,
    winners_ref,
    send,
    send_quality,
    recv_quality,
    send_winner,
    recv_winner,
    load_sem,
    fact_sem,
    send_sem,
    recv_sem,
    quality_sem,
    winner_sem,
    mate_sem,
):
    pair_size, shards, slots, width, steps, domains = sizes
    per_pair = 2 * slots // shards
    balanced = shards * per_pair
    spread_size = shards // pair_size
    group = LANES // per_pair
    groups = shards // group
    me_dp = lax.axis_index("dp")
    me_grp = lax.axis_index("grp")
    me = me_dp * pair_size + me_grp
    my_group = me // group
    my_local = me % group

    barrier = pltpu.get_barrier_semaphore()
    loads = [
        pltpu.make_async_copy(source, held, fact_sem.at[i])
        for i, (source, held) in enumerate(
            (
                (quality_hbm, quality_ref),
                (domain_hbm, domain_ref),
                (dest_hbm, dest_ref),
                (weight_hbm, weight_ref),
                (counts_hbm, counts_ref),
                (winners_hbm, winners_ref),
            )
        )
    ]
    for load in loads:
        load.start()
    load = pltpu.make_async_copy(embeds_hbm, embeds, load_sem)
    load.start()

    @pl.loop(1, shards)
    def _(k):
        peer = (me + k) % shards
        pl.semaphore_signal(
            barrier,
            inc=1,
            device_id=(peer // pair_size, peer % pair_size),
            device_id_type=MESH,
        )

    for fact_load in loads:
        fact_load.wait()

    dest = dest_ref[...]
    row = lax.broadcasted_iota(jnp.int32, (1, slots), 1)
    valid = row < counts_ref[0]
    domain = domain_ref[...]
    weight = jnp.zeros((1, slots), jnp.float32)
    for d in range(domains):
        weight = jnp.where(domain == d, weight_ref[d], weight)
    quality = jnp.where(valid, quality_ref[...] * weight, 0.0)
    quality = quality.astype(jnp.bfloat16).astype(jnp.float32)
    target = lax.broadcasted_iota(jnp.int32, (shards, slots), 0)
    hot = (target == dest) & valid
    hot_wide = jnp.where(hot, 1.0, 0.0)
    before = jnp.where(
        lax.broadcasted_iota(jnp.int32, (slots, slots), 0)
        < lax.broadcasted_iota(jnp.int32, (slots, slots), 1),
        1.0,
        0.0,
    ).astype(jnp.bfloat16)
    earlier = jnp.dot(
        hot_wide.astype(jnp.bfloat16), before, preferred_element_type=jnp.float32
    )
    rank = jnp.sum(jnp.where(hot, earlier, 0.0), axis=0, keepdims=True)
    rank = rank.astype(jnp.int32)
    slot = jnp.where(valid, dest * per_pair + rank, -1)
    place = (dest * balanced + me * per_pair + rank).astype(jnp.float32)

    lane_rank = lax.broadcasted_iota(jnp.int32, (LANES, slots), 0)
    rank_hot = jnp.where(lane_rank == rank + my_local * per_pair, 1.0, 0.0)
    spread = lax.dot_general(
        jnp.where(hot, quality, 0.0).astype(jnp.bfloat16),
        rank_hot.astype(jnp.bfloat16),
        (((1,), (1,)), ((), ())),
        preferred_element_type=jnp.float32,
    )

    chosen = row < 0
    lane = lax.broadcasted_iota(jnp.int32, (1, LANES), 1)
    lane_fact = (lane + (LANES - (my_local + 1) * per_pair)) % LANES
    meta = jnp.zeros((1, LANES), jnp.float32)
    for t in range(steps):
        local = winners_ref[t] - me * slots
        chosen_now = row == local
        chosen = chosen | chosen_now
        mine = jnp.where((local >= 0) & (local < slots), 1.0, 0.0)
        meta = jnp.where(lane_fact == t, mine, meta)
    won_quality = jnp.sum(jnp.where(chosen, quality, 0.0), axis=1, keepdims=True)
    won_place = jnp.sum(jnp.where(chosen, place, 0.0), axis=1, keepdims=True)
    meta = jnp.where(lane_fact == steps, won_quality, meta)
    meta = jnp.where(lane_fact == steps + 1, won_place, meta)
    send_quality[...] = (spread + meta).reshape(shards, 1, LANES)
    load.wait()
    picked = jnp.dot(
        jnp.broadcast_to(jnp.where(chosen, 1.0, 0.0), (16, slots)).astype(jnp.bfloat16),
        embeds[...],
        preferred_element_type=jnp.float32,
    )
    folds = width // LANES
    fold_row = lax.broadcasted_iota(jnp.int32, (folds, LANES), 0)
    folded = jnp.zeros((folds, LANES), jnp.float32)
    for f in range(folds):
        folded = jnp.where(
            fold_row == f, picked[0:1, f * LANES : (f + 1) * LANES], folded
        )
    send_winner[...] = folded.astype(jnp.bfloat16)

    slot_index = lax.broadcasted_iota(jnp.int32, (balanced, slots), 0)
    permute = jnp.where(slot_index == slot, 1.0, 0.0).astype(jnp.bfloat16)
    for c in range(0, width, 256):
        moved = jnp.dot(
            permute, embeds[:, c : c + 256], preferred_element_type=jnp.float32
        )
        send[:, :, c : c + 256] = moved.astype(jnp.bfloat16).reshape(shards, per_pair, 256)

    own_rows = pltpu.make_async_copy(send.at[me], recv.at[me], recv_sem.at[my_group])
    own_quality = pltpu.make_async_copy(
        send_quality.at[me], recv_quality.at[me], quality_sem.at[my_group]
    )
    own_winner = pltpu.make_async_copy(
        send_winner, recv_winner.at[me_grp, me_dp], winner_sem.at[0]
    )

    pl.semaphore_wait(barrier, shards - 1)

    @pl.loop(1, spread_size)
    def _(k):
        pltpu.make_async_remote_copy(
            src_ref=send_winner,
            dst_ref=recv_winner.at[me_grp, me_dp],
            send_sem=send_sem.at[0],
            recv_sem=winner_sem.at[0],
            device_id=((me_dp + k) % spread_size, me_grp),
            device_id_type=MESH,
        ).start()

    own_winner.start()

    def send_rows(bits, k):
        peer = flip(my_group, bits) * group + (my_local + k) % group
        device = (peer // pair_size, peer % pair_size)
        pltpu.make_async_remote_copy(
            src_ref=send_quality.at[peer],
            dst_ref=recv_quality.at[me],
            send_sem=send_sem.at[1],
            recv_sem=quality_sem.at[my_group],
            device_id=device,
            device_id_type=MESH,
        ).start()
        pltpu.make_async_remote_copy(
            src_ref=send.at[peer],
            dst_ref=recv.at[me],
            send_sem=send_sem.at[2],
            recv_sem=recv_sem.at[my_group],
            device_id=device,
            device_id_type=MESH,
        ).start()

    middle = groups // 2
    for bits in [middle, *(b for b in range(1, groups) if b != middle), 0]:
        @pl.loop(0 if bits else 1, group)
        def _(k):
            send_rows(bits, k)

    own_rows.start()
    own_quality.start()

    mine = recv_winner.at[me_grp]
    pltpu.make_async_copy(mine, mine, winner_sem.at[0]).wait()
    relays = []
    for k in range(1, pair_size):
        relay = pltpu.make_async_remote_copy(
            src_ref=mine,
            dst_ref=mine,
            send_sem=mate_sem.at[0, k - 1],
            recv_sem=mate_sem.at[1, k - 1],
            device_id=(me_dp, (me_grp + k) % pair_size),
            device_id_type=MESH,
        )
        relay.start()
        relays.append(relay)
    for relay in relays:
        relay.wait()
    for g in range(groups):
        scores = recv_quality.at[pl.ds(g * group, group)]
        pltpu.make_async_copy(scores, scores, quality_sem.at[g]).wait()

    facts = recv_quality[...].reshape(shards, LANES)
    source = lax.broadcasted_iota(jnp.int32, (shards, LANES), 0)
    fact_lane = lax.broadcasted_iota(jnp.int32, (shards, LANES), 1)
    fact = (fact_lane + (LANES - (source % group + 1) * per_pair)) % LANES
    def fact_of(i):
        return jnp.sum(jnp.where(fact == i, facts, 0.0), axis=1, keepdims=True)

    owners = [fact_of(t) for t in range(steps)]
    source_quality = fact_of(steps)
    source_place = fact_of(steps + 1)
    win_quality = [jnp.sum(o * source_quality, axis=0, keepdims=True) for o in owners]
    win_place = [jnp.sum(o * source_place, axis=0, keepdims=True) for o in owners]
    owner_table = jnp.zeros((shards, LANES), jnp.float32)
    for t in range(steps):
        owner_table = jnp.where(fact_lane == t, owners[t], owner_table)
    line = lax.broadcasted_iota(jnp.int32, (shards, shards * folds), 1)
    order = line // folds
    line_source = (order % spread_size) * pair_size + order // spread_size
    line_hot = jnp.where(
        line_source == lax.broadcasted_iota(jnp.int32, line.shape, 0), 1.0, 0.0
    )
    spread_owner = jnp.dot(
        owner_table.T[:16].astype(jnp.bfloat16),
        line_hot.astype(jnp.bfloat16),
        preferred_element_type=jnp.float32,
    )
    lines = recv_winner[...].reshape(shards * folds, LANES)
    line_fold = lax.broadcasted_iota(jnp.int32, spread_owner.shape, 1) % folds
    wins = jnp.concatenate(
        [
            jnp.dot(
                jnp.where(line_fold == f, spread_owner, 0.0).astype(jnp.bfloat16),
                lines,
                preferred_element_type=jnp.float32,
            )
            for f in range(folds)
        ],
        axis=1,
    ).astype(jnp.bfloat16)
    gram = lax.dot_general(
        wins, wins, (((1,), (1,)), ((), ())), preferred_element_type=jnp.float32
    )
    columns = []
    roots = []
    for t in range(steps):
        column = []
        for k in range(t):
            cross = win_quality[k] * win_quality[t] * gram[k : k + 1, t : t + 1] / width
            for e in range(k):
                cross = cross - columns[k][e] * column[e]
            column.append(cross / roots[k])
        left = win_quality[t] * win_quality[t] * gram[t : t + 1, t : t + 1] / width + RIDGE
        for k in range(t):
            left = left - column[k] * column[k]
        columns.append(column)
        roots.append(jnp.sqrt(left))

    for bits in range(groups):
        here = flip(my_group, bits)
        first = here * group
        blocks = recv.at[pl.ds(first, group)]
        scores = recv_quality.at[pl.ds(first, group)]
        pltpu.make_async_copy(blocks, blocks, recv_sem.at[here]).wait()
        rows = blocks[...].reshape(LANES, width)
        own_lane = lax.broadcasted_iota(jnp.int32, (group, LANES), 1) // per_pair
        own_lane = own_lane == lax.broadcasted_iota(jnp.int32, (group, LANES), 0)
        bal_quality = jnp.sum(
            jnp.where(own_lane, scores[...].reshape(group, LANES), 0.0),
            axis=0,
            keepdims=True,
        )
        dots = lax.dot_general(
            wins, rows, (((1,), (1,)), ((), ())), preferred_element_type=jnp.float32
        )
        total = jnp.zeros((LANES, LANES), jnp.float32)
        for c in range(0, width, LANES):
            part = rows[:, c : c + LANES].astype(jnp.float32)
            total = total + part * part
        norms = jnp.sum(total.T, axis=0, keepdims=True)
        gain = jnp.where(
            bal_quality > 0, bal_quality * bal_quality * norms / width + RIDGE, 0.0
        )
        at = (me * balanced + here * LANES + lane).astype(jnp.float32)
        span = pl.ds(pl.multiple_of(here * LANES, LANES), LANES)
        entries = []
        for t in range(steps):
            inner = jnp.zeros((1, LANES), jnp.float32)
            for k in range(t):
                inner = inner + entries[k] * columns[t][k]
            hit = jnp.where(at == win_place[t], RIDGE, 0.0)
            entry = (
                bal_quality * win_quality[t] * dots[t : t + 1] / width + hit - inner
            ) / roots[t]
            entries.append(entry)
            gain = gain - entry * entry
            chol_ref[t : t + 1, span] = entry
        gain_ref[:, span] = gain

    others = recv_winner.at[0, pl.ds(0, spread_size - 1)]
    pltpu.make_async_copy(others, others, send_sem.at[0]).wait()
    others = send_quality.at[pl.ds(0, shards - 1)]
    pltpu.make_async_copy(others, others, send_sem.at[1]).wait()
    others = send.at[pl.ds(0, shards - 1)]
    pltpu.make_async_copy(others, others, send_sem.at[2]).wait()


def write_kernel(rows, gain, chol, rows_hbm, gain_hbm, chol_hbm, sem):
    copies = [
        pltpu.make_async_copy(held, out, sem.at[i])
        for i, (held, out) in enumerate(
            ((rows, rows_hbm), (gain, gain_hbm), (chol, chol_hbm))
        )
    ]
    for copy in copies:
        copy.start()
    for copy in copies:
        copy.wait()


def body(embeds, quality, domain_ids, domain_weight, dest, counts, winners):
    shards = lax.axis_size(("dp", "grp"))
    pair_size = lax.axis_size("grp")
    slots, width = embeds.shape
    steps = winners.shape[0]
    domains = domain_weight.shape[0]
    per_pair = 2 * slots // shards
    balanced = shards * per_pair
    groups = balanced // LANES
    vmem = pl.BlockSpec(memory_space=pltpu.VMEM)
    hbm = pl.BlockSpec(memory_space=pltpu.HBM)
    dma = pltpu.SemaphoreType.DMA
    folds = width // LANES
    rows, gain, chol = pl.pallas_call(
        functools.partial(kernel, (pair_size, shards, slots, width, steps, domains)),
        out_shape=(
            pltpu.VMEM((shards, per_pair, width), jnp.bfloat16),
            pltpu.VMEM((1, balanced), jnp.float32),
            pltpu.VMEM((steps, balanced), jnp.float32),
        ),
        in_specs=[hbm] * 7,
        out_specs=(vmem, vmem, vmem),
        scratch_shapes=[
            pltpu.VMEM((slots, width), jnp.bfloat16),
            pltpu.VMEM((1, slots), jnp.float32),
            pltpu.VMEM((1, slots), jnp.int32),
            pltpu.VMEM((1, slots), jnp.int32),
            pltpu.SMEM((domains,), jnp.float32),
            pltpu.SMEM((1,), jnp.int32),
            pltpu.SMEM((steps,), jnp.int32),
            pltpu.VMEM((shards, per_pair, width), jnp.bfloat16),
            pltpu.VMEM((shards, 1, LANES), jnp.float32),
            pltpu.VMEM((shards, 1, LANES), jnp.float32),
            pltpu.VMEM((folds, LANES), jnp.bfloat16),
            pltpu.VMEM((pair_size, shards // pair_size, folds, LANES), jnp.bfloat16),
            dma,
            dma((6,)),
            dma((3,)),
            dma((groups,)),
            dma((groups,)),
            dma((1,)),
            dma((2, pair_size - 1)),
        ],
        compiler_params=pltpu.CompilerParams(
            collective_id=0, has_side_effects=True, vmem_limit_bytes=VMEM_BYTES - 1114112
        ),
        name="relay_select",
    )(
        embeds,
        quality.reshape(1, slots),
        domain_ids.reshape(1, slots),
        dest.reshape(1, slots),
        domain_weight,
        counts,
        winners,
    )
    relaid, gain, chol = pl.pallas_call(
        write_kernel,
        out_shape=(
            jax.ShapeDtypeStruct((shards, per_pair, width), jnp.bfloat16),
            jax.ShapeDtypeStruct((1, balanced), jnp.float32),
            jax.ShapeDtypeStruct((steps, balanced), jnp.float32),
        ),
        in_specs=[vmem] * 3,
        out_specs=(hbm,) * 3,
        scratch_shapes=[dma((3,))],
        compiler_params=pltpu.CompilerParams(vmem_limit_bytes=8 * 1024 * 1024),
        name="write_out",
    )(rows, gain, chol)
    return relaid.reshape(balanced, width), gain.reshape(balanced), chol


def solution(mesh):
    return jax.shard_map(
        body,
        mesh=mesh,
        in_specs=(
            P(("dp", "grp"), None),
            P(("dp", "grp")),
            P(("dp", "grp")),
            P(),
            P(("dp", "grp")),
            P(("dp", "grp")),
            P(),
        ),
        out_specs=(P(("dp", "grp"), None), P(("dp", "grp")), P(None, ("dp", "grp"))),
        check_vma=False,
    )
```

```python
import functools
import jax
import jax.numpy as jnp
from jax import lax
from jax.experimental import pallas as pl
from jax.experimental.pallas import tpu as pltpu
from jax.sharding import PartitionSpec as P

RIDGE = 0.1
VMEM_BYTES = 67043328
LANES = 128
MESH = pl.DeviceIdType.MESH


def flip(value, bits):
    out = 0
    weight = 1
    while weight <= bits:
        digit = (value // weight) % 2
        out = out + weight * ((1 - digit) if (bits // weight) % 2 else digit)
        weight *= 2
    return out + weight * (value // weight)


def kernel(
    sizes,
    embeds_hbm,
    quality_hbm,
    domain_hbm,
    dest_hbm,
    weight_hbm,
    counts_hbm,
    winners_hbm,
    recv,
    gain_ref,
    chol_ref,
    embeds,
    quality_ref,
    domain_ref,
    dest_ref,
    weight_ref,
    counts_ref,
    winners_ref,
    send,
    send_quality,
    recv_quality,
    send_winner,
    recv_winner,
    load_sem,
    fact_sem,
    send_sem,
    recv_sem,
    quality_sem,
    winner_sem,
    mate_sem,
    here_sem,
):
    pair_size, shards, slots, width, steps, domains = sizes
    per_pair = 2 * slots // shards
    balanced = shards * per_pair
    spread_size = shards // pair_size
    group = LANES // per_pair
    groups = shards // group
    me_dp = lax.axis_index("dp")
    me_grp = lax.axis_index("grp")
    me = me_dp * pair_size + me_grp
    my_group = me // group
    my_local = me % group

    barrier = pltpu.get_barrier_semaphore()
    loads = [
        pltpu.make_async_copy(source, held, fact_sem.at[i])
        for i, (source, held) in enumerate(
            (
                (quality_hbm, quality_ref),
                (domain_hbm, domain_ref),
                (dest_hbm, dest_ref),
                (weight_hbm, weight_ref),
                (counts_hbm, counts_ref),
                (winners_hbm, winners_ref),
            )
        )
    ]
    for load in loads:
        load.start()
    load = pltpu.make_async_copy(embeds_hbm, embeds, load_sem)
    load.start()

    def peer_device(bits, k):
        peer = flip(my_group, bits) * group + (my_local + k) % group
        return peer, (peer // pair_size, peer % pair_size)

    def greet(semaphore, bits, k):
        pl.semaphore_signal(
            semaphore, inc=1, device_id=peer_device(bits, k)[1], device_id_type=MESH
        )

    for bits in range(groups - 1, 0, -1):
        greet(barrier, bits, 0)

    @pl.loop(1, group)
    def _(k):
        greet(barrier, 0, k)

    for fact_load in loads:
        fact_load.wait()

    dest = dest_ref[...]
    row = lax.broadcasted_iota(jnp.int32, (1, slots), 1)
    valid = row < counts_ref[0]
    domain = domain_ref[...]
    weight = jnp.zeros((1, slots), jnp.float32)
    for d in range(domains):
        weight = jnp.where(domain == d, weight_ref[d], weight)
    quality = jnp.where(valid, quality_ref[...] * weight, 0.0)
    quality = quality.astype(jnp.bfloat16).astype(jnp.float32)
    target = lax.broadcasted_iota(jnp.int32, (shards, slots), 0)
    hot = (target == dest) & valid
    hot_wide = jnp.where(hot, 1.0, 0.0)
    before = jnp.where(
        lax.broadcasted_iota(jnp.int32, (slots, slots), 0)
        < lax.broadcasted_iota(jnp.int32, (slots, slots), 1),
        1.0,
        0.0,
    ).astype(jnp.bfloat16)
    earlier = jnp.dot(
        hot_wide.astype(jnp.bfloat16), before, preferred_element_type=jnp.float32
    )
    rank = jnp.sum(jnp.where(hot, earlier, 0.0), axis=0, keepdims=True)
    rank = rank.astype(jnp.int32)
    slot = jnp.where(valid, dest * per_pair + rank, -1)
    place = (dest * balanced + me * per_pair + rank).astype(jnp.float32)

    lane_rank = lax.broadcasted_iota(jnp.int32, (LANES, slots), 0)
    rank_hot = jnp.where(lane_rank == rank + my_local * per_pair, 1.0, 0.0)
    spread = lax.dot_general(
        jnp.where(hot, quality, 0.0).astype(jnp.bfloat16),
        rank_hot.astype(jnp.bfloat16),
        (((1,), (1,)), ((), ())),
        preferred_element_type=jnp.float32,
    )

    chosen = row < 0
    lane = lax.broadcasted_iota(jnp.int32, (1, LANES), 1)
    lane_fact = (lane + (LANES - (my_local + 1) * per_pair)) % LANES
    meta = jnp.zeros((1, LANES), jnp.float32)
    for t in range(steps):
        local = winners_ref[t] - me * slots
        chosen_now = row == local
        chosen = chosen | chosen_now
        mine = jnp.where((local >= 0) & (local < slots), 1.0, 0.0)
        meta = jnp.where(lane_fact == t, mine, meta)
    won_quality = jnp.sum(jnp.where(chosen, quality, 0.0), axis=1, keepdims=True)
    won_place = jnp.sum(jnp.where(chosen, place, 0.0), axis=1, keepdims=True)
    meta = jnp.where(lane_fact == steps, won_quality, meta)
    meta = jnp.where(lane_fact == steps + 1, won_place, meta)
    send_quality[...] = (spread + meta).reshape(shards, 1, LANES)
    load.wait()
    picked = jnp.dot(
        jnp.broadcast_to(jnp.where(chosen, 1.0, 0.0), (16, slots)).astype(jnp.bfloat16),
        embeds[...],
        preferred_element_type=jnp.float32,
    )
    folds = width // LANES
    fold_row = lax.broadcasted_iota(jnp.int32, (folds, LANES), 0)
    folded = jnp.zeros((folds, LANES), jnp.float32)
    for f in range(folds):
        folded = jnp.where(
            fold_row == f, picked[0:1, f * LANES : (f + 1) * LANES], folded
        )
    send_winner[...] = folded.astype(jnp.bfloat16)

    slot_index = lax.broadcasted_iota(jnp.int32, (balanced, slots), 0)
    permute = jnp.where(slot_index == slot, 1.0, 0.0).astype(jnp.bfloat16)
    for c in range(0, width, 256):
        moved = jnp.dot(
            permute, embeds[:, c : c + 256], preferred_element_type=jnp.float32
        )
        send[:, :, c : c + 256] = moved.astype(jnp.bfloat16).reshape(shards, per_pair, 256)

    own_rows = pltpu.make_async_copy(send.at[me], recv.at[me], recv_sem.at[my_group])
    own_quality = pltpu.make_async_copy(
        send_quality.at[me], recv_quality.at[me], quality_sem.at[my_group]
    )
    own_winner = pltpu.make_async_copy(
        send_winner, recv_winner.at[me_grp, me_dp], winner_sem.at[0]
    )

    def send_rows(bits, k):
        peer, device = peer_device(bits, k)
        pltpu.make_async_remote_copy(
            src_ref=send_quality.at[peer],
            dst_ref=recv_quality.at[me],
            send_sem=send_sem.at[1],
            recv_sem=quality_sem.at[my_group],
            device_id=device,
            device_id_type=MESH,
        ).start()
        pltpu.make_async_remote_copy(
            src_ref=send.at[peer],
            dst_ref=recv.at[me],
            send_sem=send_sem.at[2],
            recv_sem=recv_sem.at[my_group],
            device_id=device,
            device_id_type=MESH,
        ).start()

    middle = groups // 2
    away = [middle, *(b for b in range(1, groups) if b != middle)]
    pl.semaphore_wait(barrier, group - 1 + groups - 1)
    for bits in away:
        greet(here_sem, bits, 0)
    for bits in away:
        send_rows(bits, 0)
    pl.semaphore_wait(here_sem, groups - 1)

    @pl.loop(1, spread_size)
    def _(k):
        pltpu.make_async_remote_copy(
            src_ref=send_winner,
            dst_ref=recv_winner.at[me_grp, me_dp],
            send_sem=send_sem.at[0],
            recv_sem=winner_sem.at[0],
            device_id=((me_dp + k) % spread_size, me_grp),
            device_id_type=MESH,
        ).start()

    own_winner.start()

    for bits in [*away, 0]:

        @pl.loop(1, group)
        def _(k):
            send_rows(bits, k)

    own_rows.start()
    own_quality.start()

    mine = recv_winner.at[me_grp]
    pltpu.make_async_copy(mine, mine, winner_sem.at[0]).wait()
    relays = []
    for k in range(1, pair_size):
        relay = pltpu.make_async_remote_copy(
            src_ref=mine,
            dst_ref=mine,
            send_sem=mate_sem.at[0, k - 1],
            recv_sem=mate_sem.at[1, k - 1],
            device_id=(me_dp, (me_grp + k) % pair_size),
            device_id_type=MESH,
        )
        relay.start()
        relays.append(relay)
    for relay in relays:
        relay.wait()
    for g in range(groups):
        scores = recv_quality.at[pl.ds(g * group, group)]
        pltpu.make_async_copy(scores, scores, quality_sem.at[g]).wait()

    facts = recv_quality[...].reshape(shards, LANES)
    source = lax.broadcasted_iota(jnp.int32, (shards, LANES), 0)
    fact_lane = lax.broadcasted_iota(jnp.int32, (shards, LANES), 1)
    fact = (fact_lane + (LANES - (source % group + 1) * per_pair)) % LANES
    def fact_of(i):
        return jnp.sum(jnp.where(fact == i, facts, 0.0), axis=1, keepdims=True)

    owners = [fact_of(t) for t in range(steps)]
    source_quality = fact_of(steps)
    source_place = fact_of(steps + 1)
    win_quality = [jnp.sum(o * source_quality, axis=0, keepdims=True) for o in owners]
    win_place = [jnp.sum(o * source_place, axis=0, keepdims=True) for o in owners]
    owner_table = jnp.zeros((shards, LANES), jnp.float32)
    for t in range(steps):
        owner_table = jnp.where(fact_lane == t, owners[t], owner_table)
    line = lax.broadcasted_iota(jnp.int32, (shards, shards * folds), 1)
    order = line // folds
    line_source = (order % spread_size) * pair_size + order // spread_size
    line_hot = jnp.where(
        line_source == lax.broadcasted_iota(jnp.int32, line.shape, 0), 1.0, 0.0
    )
    spread_owner = jnp.dot(
        owner_table.T[:16].astype(jnp.bfloat16),
        line_hot.astype(jnp.bfloat16),
        preferred_element_type=jnp.float32,
    )
    lines = recv_winner[...].reshape(shards * folds, LANES)
    line_fold = lax.broadcasted_iota(jnp.int32, spread_owner.shape, 1) % folds
    wins = jnp.concatenate(
        [
            jnp.dot(
                jnp.where(line_fold == f, spread_owner, 0.0).astype(jnp.bfloat16),
                lines,
                preferred_element_type=jnp.float32,
            )
            for f in range(folds)
        ],
        axis=1,
    ).astype(jnp.bfloat16)
    gram = lax.dot_general(
        wins, wins, (((1,), (1,)), ((), ())), preferred_element_type=jnp.float32
    )
    columns = []
    roots = []
    for t in range(steps):
        column = []
        for k in range(t):
            cross = win_quality[k] * win_quality[t] * gram[k : k + 1, t : t + 1] / width
            for e in range(k):
                cross = cross - columns[k][e] * column[e]
            column.append(cross / roots[k])
        left = win_quality[t] * win_quality[t] * gram[t : t + 1, t : t + 1] / width + RIDGE
        for k in range(t):
            left = left - column[k] * column[k]
        columns.append(column)
        roots.append(jnp.sqrt(left))

    for bits in range(groups):
        here = flip(my_group, bits)
        first = here * group
        blocks = recv.at[pl.ds(first, group)]
        scores = recv_quality.at[pl.ds(first, group)]
        pltpu.make_async_copy(blocks, blocks, recv_sem.at[here]).wait()
        rows = blocks[...].reshape(LANES, width)
        own_lane = lax.broadcasted_iota(jnp.int32, (group, LANES), 1) // per_pair
        own_lane = own_lane == lax.broadcasted_iota(jnp.int32, (group, LANES), 0)
        bal_quality = jnp.sum(
            jnp.where(own_lane, scores[...].reshape(group, LANES), 0.0),
            axis=0,
            keepdims=True,
        )
        dots = lax.dot_general(
            wins, rows, (((1,), (1,)), ((), ())), preferred_element_type=jnp.float32
        )
        total = jnp.zeros((LANES, LANES), jnp.float32)
        for c in range(0, width, LANES):
            part = rows[:, c : c + LANES].astype(jnp.float32)
            total = total + part * part
        norms = jnp.sum(total.T, axis=0, keepdims=True)
        gain = jnp.where(
            bal_quality > 0, bal_quality * bal_quality * norms / width + RIDGE, 0.0
        )
        at = (me * balanced + here * LANES + lane).astype(jnp.float32)
        span = pl.ds(pl.multiple_of(here * LANES, LANES), LANES)
        entries = []
        for t in range(steps):
            inner = jnp.zeros((1, LANES), jnp.float32)
            for k in range(t):
                inner = inner + entries[k] * columns[t][k]
            hit = jnp.where(at == win_place[t], RIDGE, 0.0)
            entry = (
                bal_quality * win_quality[t] * dots[t : t + 1] / width + hit - inner
            ) / roots[t]
            entries.append(entry)
            gain = gain - entry * entry
            chol_ref[t : t + 1, span] = entry
        gain_ref[:, span] = gain

    others = recv_winner.at[0, pl.ds(0, spread_size - 1)]
    pltpu.make_async_copy(others, others, send_sem.at[0]).wait()
    others = send_quality.at[pl.ds(0, shards - 1)]
    pltpu.make_async_copy(others, others, send_sem.at[1]).wait()
    others = send.at[pl.ds(0, shards - 1)]
    pltpu.make_async_copy(others, others, send_sem.at[2]).wait()


def write_kernel(rows, gain, chol, rows_hbm, gain_hbm, chol_hbm, sem):
    copies = [
        pltpu.make_async_copy(held, out, sem.at[i])
        for i, (held, out) in enumerate(
            ((rows, rows_hbm), (gain, gain_hbm), (chol, chol_hbm))
        )
    ]
    for copy in copies:
        copy.start()
    for copy in copies:
        copy.wait()


def body(embeds, quality, domain_ids, domain_weight, dest, counts, winners):
    shards = lax.axis_size(("dp", "grp"))
    pair_size = lax.axis_size("grp")
    slots, width = embeds.shape
    steps = winners.shape[0]
    domains = domain_weight.shape[0]
    per_pair = 2 * slots // shards
    balanced = shards * per_pair
    groups = balanced // LANES
    vmem = pl.BlockSpec(memory_space=pltpu.VMEM)
    hbm = pl.BlockSpec(memory_space=pltpu.HBM)
    dma = pltpu.SemaphoreType.DMA
    folds = width // LANES
    rows, gain, chol = pl.pallas_call(
        functools.partial(kernel, (pair_size, shards, slots, width, steps, domains)),
        out_shape=(
            pltpu.VMEM((shards, per_pair, width), jnp.bfloat16),
            pltpu.VMEM((1, balanced), jnp.float32),
            pltpu.VMEM((steps, balanced), jnp.float32),
        ),
        in_specs=[hbm] * 7,
        out_specs=(vmem, vmem, vmem),
        scratch_shapes=[
            pltpu.VMEM((slots, width), jnp.bfloat16),
            pltpu.VMEM((1, slots), jnp.float32),
            pltpu.VMEM((1, slots), jnp.int32),
            pltpu.VMEM((1, slots), jnp.int32),
            pltpu.SMEM((domains,), jnp.float32),
            pltpu.SMEM((1,), jnp.int32),
            pltpu.SMEM((steps,), jnp.int32),
            pltpu.VMEM((shards, per_pair, width), jnp.bfloat16),
            pltpu.VMEM((shards, 1, LANES), jnp.float32),
            pltpu.VMEM((shards, 1, LANES), jnp.float32),
            pltpu.VMEM((folds, LANES), jnp.bfloat16),
            pltpu.VMEM((pair_size, shards // pair_size, folds, LANES), jnp.bfloat16),
            dma,
            dma((6,)),
            dma((3,)),
            dma((groups,)),
            dma((groups,)),
            dma((1,)),
            dma((2, pair_size - 1)),
            pltpu.SemaphoreType.REGULAR,
        ],
        compiler_params=pltpu.CompilerParams(
            collective_id=0, has_side_effects=True, vmem_limit_bytes=VMEM_BYTES - 1114112
        ),
        name="relay_select",
    )(
        embeds,
        quality.reshape(1, slots),
        domain_ids.reshape(1, slots),
        dest.reshape(1, slots),
        domain_weight,
        counts,
        winners,
    )
    relaid, gain, chol = pl.pallas_call(
        write_kernel,
        out_shape=(
            jax.ShapeDtypeStruct((shards, per_pair, width), jnp.bfloat16),
            jax.ShapeDtypeStruct((1, balanced), jnp.float32),
            jax.ShapeDtypeStruct((steps, balanced), jnp.float32),
        ),
        in_specs=[vmem] * 3,
        out_specs=(hbm,) * 3,
        scratch_shapes=[dma((3,))],
        compiler_params=pltpu.CompilerParams(vmem_limit_bytes=8 * 1024 * 1024),
        name="write_out",
    )(rows, gain, chol)
    return relaid.reshape(balanced, width), gain.reshape(balanced), chol


def solution(mesh):
    return jax.shard_map(
        body,
        mesh=mesh,
        in_specs=(
            P(("dp", "grp"), None),
            P(("dp", "grp")),
            P(("dp", "grp")),
            P(),
            P(("dp", "grp")),
            P(("dp", "grp")),
            P(),
        ),
        out_specs=(P(("dp", "grp"), None), P(("dp", "grp")), P(None, ("dp", "grp"))),
        check_vma=False,
    )
```

```python
import functools
import jax
import jax.numpy as jnp
from jax import lax
from jax.experimental import pallas as pl
from jax.experimental.pallas import tpu as pltpu
from jax.sharding import PartitionSpec as P

RIDGE = 0.1
VMEM_BYTES = 67043328
LANES = 128
MESH = pl.DeviceIdType.MESH


def flip(value, bits):
    out = 0
    weight = 1
    while weight <= bits:
        digit = (value // weight) % 2
        out = out + weight * ((1 - digit) if (bits // weight) % 2 else digit)
        weight *= 2
    return out + weight * (value // weight)


def kernel(
    sizes,
    embeds_hbm,
    quality_hbm,
    domain_hbm,
    dest_hbm,
    weight_hbm,
    counts_hbm,
    winners_hbm,
    recv,
    gain_ref,
    chol_ref,
    embeds,
    quality_ref,
    domain_ref,
    dest_ref,
    weight_ref,
    counts_ref,
    winners_ref,
    send,
    send_quality,
    recv_quality,
    send_winner,
    recv_winner,
    load_sem,
    fact_sem,
    send_sem,
    recv_sem,
    quality_sem,
    winner_sem,
    mate_sem,
    here_sem,
):
    pair_size, shards, slots, width, steps, domains = sizes
    per_pair = 2 * slots // shards
    balanced = shards * per_pair
    spread_size = shards // pair_size
    group = LANES // per_pair
    groups = shards // group
    me_dp = lax.axis_index("dp")
    me_grp = lax.axis_index("grp")
    me = me_dp * pair_size + me_grp
    my_group = me // group
    my_local = me % group

    barrier = pltpu.get_barrier_semaphore()
    def peer_device(bits, k):
        peer = flip(my_group, bits) * group + (my_local + k) % group
        return peer, (peer // pair_size, peer % pair_size)

    def greet(semaphore, bits, k):
        pl.semaphore_signal(
            semaphore, inc=1, device_id=peer_device(bits, k)[1], device_id_type=MESH
        )

    for bits in range(groups - 1, 0, -1):
        greet(barrier, bits, 0)

    @pl.loop(1, group)
    def _(k):
        greet(barrier, 0, k)

    loads = [
        pltpu.make_async_copy(source, held, fact_sem.at[i])
        for i, (source, held) in enumerate(
            (
                (quality_hbm, quality_ref),
                (domain_hbm, domain_ref),
                (dest_hbm, dest_ref),
                (weight_hbm, weight_ref),
                (counts_hbm, counts_ref),
                (winners_hbm, winners_ref),
            )
        )
    ]
    for load in loads:
        load.start()
    load = pltpu.make_async_copy(embeds_hbm, embeds, load_sem)
    load.start()

    for fact_load in loads:
        fact_load.wait()

    dest = dest_ref[...]
    row = lax.broadcasted_iota(jnp.int32, (1, slots), 1)
    valid = row < counts_ref[0]
    domain = domain_ref[...]
    weight = jnp.zeros((1, slots), jnp.float32)
    for d in range(domains):
        weight = jnp.where(domain == d, weight_ref[d], weight)
    quality = jnp.where(valid, quality_ref[...] * weight, 0.0)
    quality = quality.astype(jnp.bfloat16).astype(jnp.float32)
    target = lax.broadcasted_iota(jnp.int32, (shards, slots), 0)
    hot = (target == dest) & valid
    hot_wide = jnp.where(hot, 1.0, 0.0)
    before = jnp.where(
        lax.broadcasted_iota(jnp.int32, (slots, slots), 0)
        < lax.broadcasted_iota(jnp.int32, (slots, slots), 1),
        1.0,
        0.0,
    ).astype(jnp.bfloat16)
    earlier = jnp.dot(
        hot_wide.astype(jnp.bfloat16), before, preferred_element_type=jnp.float32
    )
    rank = jnp.sum(jnp.where(hot, earlier, 0.0), axis=0, keepdims=True)
    rank = rank.astype(jnp.int32)
    slot = jnp.where(valid, dest * per_pair + rank, -1)
    place = (dest * balanced + me * per_pair + rank).astype(jnp.float32)

    lane_rank = lax.broadcasted_iota(jnp.int32, (LANES, slots), 0)
    rank_hot = jnp.where(lane_rank == rank + my_local * per_pair, 1.0, 0.0)
    spread = lax.dot_general(
        jnp.where(hot, quality, 0.0).astype(jnp.bfloat16),
        rank_hot.astype(jnp.bfloat16),
        (((1,), (1,)), ((), ())),
        preferred_element_type=jnp.float32,
    )

    chosen = row < 0
    lane = lax.broadcasted_iota(jnp.int32, (1, LANES), 1)
    lane_fact = (lane + (LANES - (my_local + 1) * per_pair)) % LANES
    meta = jnp.zeros((1, LANES), jnp.float32)
    for t in range(steps):
        local = winners_ref[t] - me * slots
        chosen_now = row == local
        chosen = chosen | chosen_now
        mine = jnp.where((local >= 0) & (local < slots), 1.0, 0.0)
        meta = jnp.where(lane_fact == t, mine, meta)
    won_quality = jnp.sum(jnp.where(chosen, quality, 0.0), axis=1, keepdims=True)
    won_place = jnp.sum(jnp.where(chosen, place, 0.0), axis=1, keepdims=True)
    meta = jnp.where(lane_fact == steps, won_quality, meta)
    meta = jnp.where(lane_fact == steps + 1, won_place, meta)
    send_quality[...] = (spread + meta).reshape(shards, 1, LANES)
    load.wait()
    picked = jnp.dot(
        jnp.broadcast_to(jnp.where(chosen, 1.0, 0.0), (16, slots)).astype(jnp.bfloat16),
        embeds[...],
        preferred_element_type=jnp.float32,
    )
    folds = width // LANES
    fold_row = lax.broadcasted_iota(jnp.int32, (folds, LANES), 0)
    folded = jnp.zeros((folds, LANES), jnp.float32)
    for f in range(folds):
        folded = jnp.where(
            fold_row == f, picked[0:1, f * LANES : (f + 1) * LANES], folded
        )
    send_winner[...] = folded.astype(jnp.bfloat16)

    slot_index = lax.broadcasted_iota(jnp.int32, (balanced, slots), 0)
    permute = jnp.where(slot_index == slot, 1.0, 0.0).astype(jnp.bfloat16)
    for c in range(0, width, 256):
        moved = jnp.dot(
            permute, embeds[:, c : c + 256], preferred_element_type=jnp.float32
        )
        send[:, :, c : c + 256] = moved.astype(jnp.bfloat16).reshape(shards, per_pair, 256)

    own_rows = pltpu.make_async_copy(send.at[me], recv.at[me], recv_sem.at[my_group])
    own_quality = pltpu.make_async_copy(
        send_quality.at[me], recv_quality.at[me], quality_sem.at[my_group]
    )
    own_winner = pltpu.make_async_copy(
        send_winner, recv_winner.at[me_grp, me_dp], winner_sem.at[0]
    )

    def send_rows(bits, k):
        peer, device = peer_device(bits, k)
        pltpu.make_async_remote_copy(
            src_ref=send_quality.at[peer],
            dst_ref=recv_quality.at[me],
            send_sem=send_sem.at[1],
            recv_sem=quality_sem.at[my_group],
            device_id=device,
            device_id_type=MESH,
        ).start()
        pltpu.make_async_remote_copy(
            src_ref=send.at[peer],
            dst_ref=recv.at[me],
            send_sem=send_sem.at[2],
            recv_sem=recv_sem.at[my_group],
            device_id=device,
            device_id_type=MESH,
        ).start()

    middle = groups // 2
    away = [middle, *(b for b in range(1, groups) if b != middle)]
    pl.semaphore_wait(barrier, group - 1 + groups - 1)
    for bits in away:
        greet(here_sem, bits, 0)
    for bits in away:
        send_rows(bits, 0)
    pl.semaphore_wait(here_sem, groups - 1)

    @pl.loop(1, spread_size)
    def _(k):
        pltpu.make_async_remote_copy(
            src_ref=send_winner,
            dst_ref=recv_winner.at[me_grp, me_dp],
            send_sem=send_sem.at[0],
            recv_sem=winner_sem.at[0],
            device_id=((me_dp + k) % spread_size, me_grp),
            device_id_type=MESH,
        ).start()

    own_winner.start()

    for bits in [*away, 0]:

        @pl.loop(1, group)
        def _(k):
            send_rows(bits, k)

    own_rows.start()
    own_quality.start()

    mine = recv_winner.at[me_grp]
    pltpu.make_async_copy(mine, mine, winner_sem.at[0]).wait()
    relays = []
    for k in range(1, pair_size):
        relay = pltpu.make_async_remote_copy(
            src_ref=mine,
            dst_ref=mine,
            send_sem=mate_sem.at[0, k - 1],
            recv_sem=mate_sem.at[1, k - 1],
            device_id=(me_dp, (me_grp + k) % pair_size),
            device_id_type=MESH,
        )
        relay.start()
        relays.append(relay)
    for relay in relays:
        relay.wait()
    for g in range(groups):
        scores = recv_quality.at[pl.ds(g * group, group)]
        pltpu.make_async_copy(scores, scores, quality_sem.at[g]).wait()

    facts = recv_quality[...].reshape(shards, LANES)
    source = lax.broadcasted_iota(jnp.int32, (shards, LANES), 0)
    fact_lane = lax.broadcasted_iota(jnp.int32, (shards, LANES), 1)
    fact = (fact_lane + (LANES - (source % group + 1) * per_pair)) % LANES
    def fact_of(i):
        return jnp.sum(jnp.where(fact == i, facts, 0.0), axis=1, keepdims=True)

    owners = [fact_of(t) for t in range(steps)]
    source_quality = fact_of(steps)
    source_place = fact_of(steps + 1)
    win_quality = [jnp.sum(o * source_quality, axis=0, keepdims=True) for o in owners]
    win_place = [jnp.sum(o * source_place, axis=0, keepdims=True) for o in owners]
    owner_table = jnp.zeros((shards, LANES), jnp.float32)
    for t in range(steps):
        owner_table = jnp.where(fact_lane == t, owners[t], owner_table)
    line = lax.broadcasted_iota(jnp.int32, (shards, shards * folds), 1)
    order = line // folds
    line_source = (order % spread_size) * pair_size + order // spread_size
    line_hot = jnp.where(
        line_source == lax.broadcasted_iota(jnp.int32, line.shape, 0), 1.0, 0.0
    )
    spread_owner = jnp.dot(
        owner_table.T[:16].astype(jnp.bfloat16),
        line_hot.astype(jnp.bfloat16),
        preferred_element_type=jnp.float32,
    )
    lines = recv_winner[...].reshape(shards * folds, LANES)
    line_fold = lax.broadcasted_iota(jnp.int32, spread_owner.shape, 1) % folds
    wins = jnp.concatenate(
        [
            jnp.dot(
                jnp.where(line_fold == f, spread_owner, 0.0).astype(jnp.bfloat16),
                lines,
                preferred_element_type=jnp.float32,
            )
            for f in range(folds)
        ],
        axis=1,
    ).astype(jnp.bfloat16)
    gram = lax.dot_general(
        wins, wins, (((1,), (1,)), ((), ())), preferred_element_type=jnp.float32
    )
    columns = []
    roots = []
    for t in range(steps):
        column = []
        for k in range(t):
            cross = win_quality[k] * win_quality[t] * gram[k : k + 1, t : t + 1] / width
            for e in range(k):
                cross = cross - columns[k][e] * column[e]
            column.append(cross / roots[k])
        left = win_quality[t] * win_quality[t] * gram[t : t + 1, t : t + 1] / width + RIDGE
        for k in range(t):
            left = left - column[k] * column[k]
        columns.append(column)
        roots.append(jnp.sqrt(left))

    for bits in range(groups):
        here = flip(my_group, bits)
        first = here * group
        blocks = recv.at[pl.ds(first, group)]
        scores = recv_quality.at[pl.ds(first, group)]
        pltpu.make_async_copy(blocks, blocks, recv_sem.at[here]).wait()
        rows = blocks[...].reshape(LANES, width)
        own_lane = lax.broadcasted_iota(jnp.int32, (group, LANES), 1) // per_pair
        own_lane = own_lane == lax.broadcasted_iota(jnp.int32, (group, LANES), 0)
        bal_quality = jnp.sum(
            jnp.where(own_lane, scores[...].reshape(group, LANES), 0.0),
            axis=0,
            keepdims=True,
        )
        dots = lax.dot_general(
            wins, rows, (((1,), (1,)), ((), ())), preferred_element_type=jnp.float32
        )
        total = jnp.zeros((LANES, LANES), jnp.float32)
        for c in range(0, width, LANES):
            part = rows[:, c : c + LANES].astype(jnp.float32)
            total = total + part * part
        norms = jnp.sum(total.T, axis=0, keepdims=True)
        gain = jnp.where(
            bal_quality > 0, bal_quality * bal_quality * norms / width + RIDGE, 0.0
        )
        at = (me * balanced + here * LANES + lane).astype(jnp.float32)
        span = pl.ds(pl.multiple_of(here * LANES, LANES), LANES)
        entries = []
        for t in range(steps):
            inner = jnp.zeros((1, LANES), jnp.float32)
            for k in range(t):
                inner = inner + entries[k] * columns[t][k]
            hit = jnp.where(at == win_place[t], RIDGE, 0.0)
            entry = (
                bal_quality * win_quality[t] * dots[t : t + 1] / width + hit - inner
            ) / roots[t]
            entries.append(entry)
            gain = gain - entry * entry
            chol_ref[t : t + 1, span] = entry
        gain_ref[:, span] = gain

    others = recv_winner.at[0, pl.ds(0, spread_size - 1)]
    pltpu.make_async_copy(others, others, send_sem.at[0]).wait()
    others = send_quality.at[pl.ds(0, shards - 1)]
    pltpu.make_async_copy(others, others, send_sem.at[1]).wait()
    others = send.at[pl.ds(0, shards - 1)]
    pltpu.make_async_copy(others, others, send_sem.at[2]).wait()


def write_kernel(rows, gain, chol, rows_hbm, gain_hbm, chol_hbm, sem):
    quarter = rows.shape[0] // 4
    parts = [pl.ds(i * quarter, quarter) for i in range(4)]
    pairs = [(rows.at[part], rows_hbm.at[part]) for part in parts]
    pairs += [(gain, gain_hbm), (chol, chol_hbm)]
    copies = [
        pltpu.make_async_copy(held, out, sem.at[i])
        for i, (held, out) in enumerate(pairs)
    ]
    for copy in copies:
        copy.start()
    for copy in copies:
        copy.wait()


def body(embeds, quality, domain_ids, domain_weight, dest, counts, winners):
    shards = lax.axis_size(("dp", "grp"))
    pair_size = lax.axis_size("grp")
    slots, width = embeds.shape
    steps = winners.shape[0]
    domains = domain_weight.shape[0]
    per_pair = 2 * slots // shards
    balanced = shards * per_pair
    groups = balanced // LANES
    vmem = pl.BlockSpec(memory_space=pltpu.VMEM)
    hbm = pl.BlockSpec(memory_space=pltpu.HBM)
    dma = pltpu.SemaphoreType.DMA
    folds = width // LANES
    rows, gain, chol = pl.pallas_call(
        functools.partial(kernel, (pair_size, shards, slots, width, steps, domains)),
        out_shape=(
            pltpu.VMEM((shards, per_pair, width), jnp.bfloat16),
            pltpu.VMEM((1, balanced), jnp.float32),
            pltpu.VMEM((steps, balanced), jnp.float32),
        ),
        in_specs=[hbm] * 7,
        out_specs=(vmem, vmem, vmem),
        scratch_shapes=[
            pltpu.VMEM((slots, width), jnp.bfloat16),
            pltpu.VMEM((1, slots), jnp.float32),
            pltpu.VMEM((1, slots), jnp.int32),
            pltpu.VMEM((1, slots), jnp.int32),
            pltpu.SMEM((domains,), jnp.float32),
            pltpu.SMEM((1,), jnp.int32),
            pltpu.SMEM((steps,), jnp.int32),
            pltpu.VMEM((shards, per_pair, width), jnp.bfloat16),
            pltpu.VMEM((shards, 1, LANES), jnp.float32),
            pltpu.VMEM((shards, 1, LANES), jnp.float32),
            pltpu.VMEM((folds, LANES), jnp.bfloat16),
            pltpu.VMEM((pair_size, shards // pair_size, folds, LANES), jnp.bfloat16),
            dma,
            dma((6,)),
            dma((3,)),
            dma((groups,)),
            dma((groups,)),
            dma((1,)),
            dma((2, pair_size - 1)),
            pltpu.SemaphoreType.REGULAR,
        ],
        compiler_params=pltpu.CompilerParams(
            collective_id=0, has_side_effects=True, vmem_limit_bytes=VMEM_BYTES - 1114112
        ),
        name="relay_select",
    )(
        embeds,
        quality.reshape(1, slots),
        domain_ids.reshape(1, slots),
        dest.reshape(1, slots),
        domain_weight,
        counts,
        winners,
    )
    relaid, gain, chol = pl.pallas_call(
        write_kernel,
        out_shape=(
            jax.ShapeDtypeStruct((shards, per_pair, width), jnp.bfloat16),
            jax.ShapeDtypeStruct((1, balanced), jnp.float32),
            jax.ShapeDtypeStruct((steps, balanced), jnp.float32),
        ),
        in_specs=[vmem] * 3,
        out_specs=(hbm,) * 3,
        scratch_shapes=[dma((6,))],
        compiler_params=pltpu.CompilerParams(vmem_limit_bytes=8 * 1024 * 1024),
        name="write_out",
    )(rows, gain, chol)
    return relaid.reshape(balanced, width), gain.reshape(balanced), chol


def solution(mesh):
    return jax.shard_map(
        body,
        mesh=mesh,
        in_specs=(
            P(("dp", "grp"), None),
            P(("dp", "grp")),
            P(("dp", "grp")),
            P(),
            P(("dp", "grp")),
            P(("dp", "grp")),
            P(),
        ),
        out_specs=(P(("dp", "grp"), None), P(("dp", "grp")), P(None, ("dp", "grp"))),
        check_vma=False,
    )
```
